32 devices in a mesh: row: 4 (over z), col: 8 (over y, x, core).
Axes of the slice: x: 2, y: 2, z: 4, core: 2. Of those that a mesh axis runs over, the one named last changes fastest.
Arguments:
- inputs: bfloat16 [192, 12288], P('col', 'row'), may hold values from -40 to 40
- ln_gain: float32 [12288], P('row'), may hold values from 0.25 to 1.75
- ln_bias: float32 [12288], P('row'), may hold values from -4 to 4
- w_up: bfloat16 [12288, 49152], P('row', 'col'), may hold values from -0.0546875 to 0.0546875
- up_bias: float32 [49152], P('col'), may hold values from -4 to 4
- w_down: bfloat16 [49152, 12288], P('col', 'row'), may hold values from -0.02734375 to 0.02734375
- down_bias: float32 [12288], P('row'), may hold values from -4 to 4
Outputs:
- block_out: bfloat16 [192, 12288], P('col', 'row')
The draws below stay inside these ranges and needn't reach their ends.
All inputs are finite; a program needn't handle non-finite values.
Results may differ from the reference program's by a relative error of at most 0.0085.
Values may be sent and summed in bfloat16 or wider, within the bound.
No kernel may reach another device: no remote copies, remote signals or barrier semaphores. Data moves between devices by JAX's collectives and lax.ppermute only.
A program may use at most 128 MiB of HBM per device.

```python
import math
import jax
import jax.numpy as jnp
from jax import lax

D = 12288
FFW = 49152
TOKENS = 192
N_ROW = 4
N_COL = 8


def draw_inputs(key, part):
    key_base = jax.random.fold_in(key, 11)
    key_jitter = jax.random.fold_in(key, 12)
    key_rows = jax.random.fold_in(key, 13)
    key_offset = jax.random.fold_in(key, 14)
    key_sign = jax.random.fold_in(key, 15)
    key_start = jax.random.fold_in(key, 16)
    key_band_sign = jax.random.fold_in(key, 17)
    key_band_size = jax.random.fold_in(key, 18)
    position = jnp.arange(D, dtype=jnp.float32) / (D - 1)
    jitter = jax.random.uniform(key_jitter, (D,), jnp.float32, 0.0, math.log(3.3))
    col_scale = jnp.exp(math.log(3.0) * (position - 0.5) + jitter - 0.5 * math.log(3.3))
    row_scale = jnp.exp(jax.random.uniform(key_rows, (TOKENS, 1), jnp.float32, math.log(0.3), math.log(3.0)))
    sign = jnp.where(jax.random.uniform(key_sign, (TOKENS, 1), jnp.float32) < 0.5, -1.0, 1.0)
    band_width = max(D // 64, 1)
    band_count = D // band_width
    band_start = jax.random.randint(key_start, (), 0, band_count, dtype=jnp.int32) * band_width
    feature = jnp.arange(D, dtype=jnp.int32)
    in_band = jnp.logical_and(feature >= band_start, feature < band_start + band_width)
    band_sign = jnp.where(jax.random.uniform(key_band_sign, (TOKENS, 1), jnp.float32) < 0.5, -1.0, 1.0)
    base = jnp.clip(jax.random.normal(key_base, (TOKENS, D), jnp.float32), -3.5, 3.5)
    level = sign * jax.random.uniform(key_offset, (TOKENS, 1), jnp.float32, 0.5, 1.5)
    values = base * row_scale * col_scale + level * (1.0 + 2.0 * position)
    band_size = jax.random.uniform(key_band_size, (TOKENS, D), jnp.float32, 0.85, 1.2)
    band_values = band_sign * 10.0 * row_scale * band_size
    values = jnp.where(in_band[None, :], band_values, values)
    return values.astype(jnp.bfloat16)


def block_levels(stream_key, extent, pieces, low, high):
    factor_of, own = 1.0, jax.random.fold_in(stream_key, 6)
    for dim, parts in pieces:
        heights = jnp.exp(jax.random.uniform(jax.random.fold_in(own, dim), (parts,), jnp.float32, low / len(pieces), high / len(pieces)))
        factor_of = factor_of * jnp.repeat(heights, extent[dim] // parts).reshape([-1 if axis == dim else 1 for axis in range(len(extent))])
    return factor_of


def gaussian(own_key, extent, width, reach, shards=(), held_as=jnp.bfloat16):
    result = jax.random.normal(own_key, extent, jnp.float32) * width
    if len(shards) > 0:
        result = block_levels(own_key, extent, shards, -0.22, 0.18) * result
    return jnp.clip(result, min=-reach, max=reach).astype(held_as)


def setup_inputs(seed: int = 0) -> dict:
    seeds = jax.random.split(jax.random.key(seed), 8)
    return {
        "inputs": draw_inputs(jax.random.fold_in(seeds[7], 71), 0),
        "ln_gain": jnp.clip(1.0 + 0.15 * jax.random.normal(seeds[1], (D,), jnp.float32), 0.25, 1.75),
        "ln_bias": gaussian(seeds[2], (D,), 0.3, 4.0, ((0, 4),), jnp.float32),
        "w_up": gaussian(seeds[3], (D, FFW), D ** -0.5, 0.0546875, ((0, 4), (1, 8))),
        "up_bias": gaussian(seeds[4], (FFW,), 0.5, 4.0, ((0, 8),), jnp.float32),
        "w_down": gaussian(seeds[5], (FFW, D), FFW ** -0.5, 0.02734375, ((0, 8), (1, 4))),
        "down_bias": gaussian(seeds[6], (D,), 0.5, 4.0, ((0, 4),), jnp.float32),
    }


def reference(inputs, ln_gain, ln_bias, w_up, up_bias, w_down, down_bias):
    in_float = inputs.astype(jnp.float32)
    average = lax.optimization_barrier(jnp.sum(in_float, axis=1, keepdims=True)) / D
    centered = in_float - average
    variance = lax.optimization_barrier(jnp.sum(centered * centered, axis=1, keepdims=True)) / D
    normed = (centered * lax.rsqrt(variance + 1e-05) * ln_gain + ln_bias).astype(jnp.bfloat16)
    feat_block = D // N_ROW

    def up_step(accumulated, block_index):
        offset = (block_index * feat_block).astype(jnp.int32)
        left_part = lax.dynamic_slice_in_dim(normed, offset, feat_block, 1)
        right_part = lax.dynamic_slice_in_dim(w_up, offset, feat_block, 0)
        partial_value = jnp.dot(left_part, right_part, preferred_element_type=jnp.float32)
        partial_value = lax.optimization_barrier(partial_value.astype(jnp.bfloat16)).astype(jnp.float32)
        return (accumulated + partial_value, None)
    up_sum, _ = lax.scan(up_step, jnp.zeros((TOKENS, FFW), jnp.float32), jnp.arange(N_ROW, dtype=jnp.int32))
    hidden = jax.nn.gelu(up_sum + up_bias, approximate=True).astype(jnp.bfloat16)
    unit_block = FFW // N_COL

    def down_step(accumulated, block_index):
        offset = (block_index * unit_block).astype(jnp.int32)
        left_part = lax.dynamic_slice_in_dim(hidden, offset, unit_block, 1)
        right_part = lax.dynamic_slice_in_dim(w_down, offset, unit_block, 0)
        partial_value = jnp.dot(left_part, right_part, preferred_element_type=jnp.float32)
        partial_value = lax.optimization_barrier(partial_value.astype(jnp.bfloat16)).astype(jnp.float32)
        return (accumulated + partial_value, None)
    down_sum, _ = lax.scan(down_step, jnp.zeros((TOKENS, D), jnp.float32), jnp.arange(N_COL, dtype=jnp.int32))
    return (in_float + down_sum + down_bias).astype(jnp.bfloat16)
```

```python
import functools
import math

import jax
import jax.numpy as jnp
from jax import lax
from jax.sharding import PartitionSpec as P

CHUNKS = 6


class Grid:
    def __init__(self, n_row, n_col):
        self.n_row, self.n_col = n_row, n_col
        self.cores = 2
        self.side = math.isqrt(n_col // self.cores)

    def shifted(self, index, dy, dx, dc):
        y, rest = divmod(index, self.side * self.cores)
        x, core = divmod(rest, self.cores)
        y, x = (y + dy) % self.side, (x + dx) % self.side
        core = (core + dc) % self.cores
        return (y * self.side + x) * self.cores + core

    def take(self, value, dy, dx, dc):
        pairs = [(self.shifted(i, dy, dx, dc), i) for i in range(self.n_col)]
        return lax.ppermute(value, "col", pairs)

    def give(self, value, dy, dx, dc):
        pairs = [(i, self.shifted(i, dy, dx, dc)) for i in range(self.n_col)]
        return lax.ppermute(value, "col", pairs)

    def turn(self, value, step):
        pairs = []
        for i in range(self.n_col):
            far = (step, 0, 0) if i % self.cores == 0 else (0, step, 0)
            pairs.append((self.shifted(i, *far), i))
        return lax.ppermute(value, "col", pairs)


def row_sum(grid, value):
    total = value
    for step in range(1, grid.n_row):
        pairs = [(i, (i + step) % grid.n_row) for i in range(grid.n_row)]
        total = total + lax.ppermute(value, "row", pairs)
    return total


def gather(grid, own):
    side = grid.side
    core = lax.axis_index("col") % grid.cores
    along_x = [grid.take(own, 0, d, 0) for d in range(1, side)]
    along_y = [grid.take(own, d, 0, 0) for d in range(1, side)]
    turned = jnp.where(core == 0, jnp.concatenate(along_x), jnp.concatenate(along_y))
    rows = own.shape[0]
    far = {}
    for step in range(1, side):
        block = grid.turn(turned, step)
        for d in range(1, side):
            far[step, d] = block[(d - 1) * rows : d * rows]
    held = []
    for dy in range(side):
        for dx in range(side):
            if dy == 0 and dx == 0:
                held.append(own)
            elif dy == 0:
                held.append(along_x[dx - 1])
            elif dx == 0:
                held.append(along_y[dy - 1])
            else:
                first, second = far[dy, dx], far[dx, dy]
                held.append(first if side == 2 else jnp.where(core == 0, first, second))
    held = jnp.concatenate(held)
    return jnp.concatenate([held, grid.take(held, 0, 0, 1)])


def scatter_sum(grid, terms):
    half = terms.shape[0] // grid.cores
    other = grid.give(terms[half:].astype(jnp.bfloat16), 0, 0, 1)
    pair = terms[:half] + other.astype(jnp.float32)
    rows = half // (grid.side * grid.side)
    total = pair[:rows]
    sent = pair.astype(jnp.bfloat16)
    for k in range(1, grid.side * grid.side):
        dy, dx = divmod(k, grid.side)
        total = total + grid.give(sent[k * rows : (k + 1) * rows], dy, dx, 0).astype(jnp.float32)
    return total


def local(grid, inputs, ln_gain, ln_bias, w_up, up_bias, w_down, down_bias):
    n_row = grid.n_row
    width = inputs.shape[1] * n_row
    in_float = inputs.astype(jnp.float32)
    sums = jnp.stack([jnp.sum(in_float, axis=1), jnp.sum(in_float * in_float, axis=1)])
    total = row_sum(grid, sums)
    average = total[0] / width
    variance = total[1] / width - average * average
    normed = (in_float - average[:, None]) * lax.rsqrt(variance + 1e-05)[:, None]
    normed = (normed * ln_gain + ln_bias).astype(jnp.bfloat16)
    gathered = gather(grid, normed)

    tokens, units = gathered.shape[0], w_up.shape[1]
    half = tokens // 2
    row = lax.axis_index("row")
    middle = n_row // 2
    upper = row >= middle
    depth = jnp.where(upper, n_row - 1 - row, row)
    inward = [(i, i + 1) for i in range(middle - 1)] + [(i, i - 1) for i in range(middle + 1, n_row)]
    outward = [(j, i) for i, j in inward]
    across = [(middle - 1, middle), (middle, middle - 1)]

    count = min(CHUNKS, units // 128)
    edges = [units // 128 * k // count * 128 for k in range(count)] + [units]
    own_of = lambda v: jnp.where(upper, v[half:], v[:half])
    other_of = lambda v: jnp.where(upper, v[:half], v[half:])

    terms = jnp.zeros((tokens, w_down.shape[1]), jnp.float32)
    own_before = None
    out_before = None
    for k in range(count + 1):
        parts = []
        if k < count:
            low, high = edges[k], edges[k + 1]
            partial = jnp.dot(gathered, w_up[:, low:high], preferred_element_type=jnp.float32)
            partial = partial.astype(jnp.bfloat16)
            acc = partial
            for _ in range(middle - 1):
                acc = partial.astype(jnp.float32) + lax.ppermute(acc, "row", inward).astype(jnp.float32)
                acc = acc.astype(jnp.bfloat16)
            parts.append(other_of(acc))
        if k > 0:
            parts.append(own_before)
        crossed = lax.ppermute(jnp.concatenate(parts, axis=1), "row", across)
        out = []
        if k < count:
            summed = own_of(acc).astype(jnp.float32) + crossed[:, : high - low].astype(jnp.float32)
            hidden = jax.nn.gelu(summed + up_bias[low:high], approximate=True).astype(jnp.bfloat16)
            out.append(hidden)
        if k > 0:
            out.append(crossed[:, crossed.shape[1] - own_before.shape[1] :])
        out = jnp.concatenate(out, axis=1)
        for hop in range(middle - 1):
            got = lax.ppermute(out, "row", outward)
            out = jnp.where(depth == middle - 2 - hop, got, out)
        if k > 0:
            before, now = edges[k - 1], edges[k]
            mine = out_before[:, : now - before]
            theirs = out[:, out.shape[1] - (now - before) :]
            lower = jnp.where(upper, theirs, mine)
            higher = jnp.where(upper, mine, theirs)
            terms = terms + jnp.dot(
                jnp.concatenate([lower, higher]), w_down[before:now], preferred_element_type=jnp.float32
            )
        if k < count:
            own_before, out_before = hidden, out
    down_sum = scatter_sum(grid, terms)
    return (in_float + down_sum + down_bias).astype(jnp.bfloat16)


def solution(mesh):
    grid = Grid(mesh.shape["row"], mesh.shape["col"])
    placed = (
        P("col", "row"),
        P("row"),
        P("row"),
        P("row", "col"),
        P("col"),
        P("col", "row"),
        P("row"),
    )
    return jax.shard_map(
        functools.partial(local, grid), mesh=mesh, in_specs=placed, out_specs=P("col", "row"), check_vma=False
    )
```

```python
import functools
import math

import jax
import jax.numpy as jnp
from jax import lax
from jax.sharding import PartitionSpec as P

SHARES = (4, 4, 4, 4, 4, 4)


class Grid:
    def __init__(self, n_row, n_col):
        self.n_row, self.n_col = n_row, n_col
        self.cores = 2
        self.side = math.isqrt(n_col // self.cores)

    def shifted(self, index, dy, dx, dc):
        y, rest = divmod(index, self.side * self.cores)
        x, core = divmod(rest, self.cores)
        y, x = (y + dy) % self.side, (x + dx) % self.side
        core = (core + dc) % self.cores
        return (y * self.side + x) * self.cores + core

    def take(self, value, dy, dx, dc):
        pairs = [(self.shifted(i, dy, dx, dc), i) for i in range(self.n_col)]
        return lax.ppermute(value, "col", pairs)

    def give(self, value, dy, dx, dc):
        pairs = [(i, self.shifted(i, dy, dx, dc)) for i in range(self.n_col)]
        return lax.ppermute(value, "col", pairs)

    def turn(self, value, step):
        pairs = []
        for i in range(self.n_col):
            far = (step, 0, 0) if i % self.cores == 0 else (0, step, 0)
            pairs.append((self.shifted(i, *far), i))
        return lax.ppermute(value, "col", pairs)


def row_sum(grid, value):
    total = value
    for step in range(1, grid.n_row):
        pairs = [(i, (i + step) % grid.n_row) for i in range(grid.n_row)]
        total = total + lax.ppermute(value, "row", pairs)
    return total


def gather(grid, own):
    side = grid.side
    core = lax.axis_index("col") % grid.cores
    along_x = [grid.take(own, 0, d, 0) for d in range(1, side)]
    along_y = [grid.take(own, d, 0, 0) for d in range(1, side)]
    turned = jnp.where(core == 0, jnp.concatenate(along_x), jnp.concatenate(along_y))
    rows = own.shape[0]
    far = {}
    for step in range(1, side):
        block = grid.turn(turned, step)
        for d in range(1, side):
            far[step, d] = block[(d - 1) * rows : d * rows]
    held = []
    for dy in range(side):
        for dx in range(side):
            if dy == 0 and dx == 0:
                held.append(own)
            elif dy == 0:
                held.append(along_x[dx - 1])
            elif dx == 0:
                held.append(along_y[dy - 1])
            else:
                first, second = far[dy, dx], far[dx, dy]
                held.append(first if side == 2 else jnp.where(core == 0, first, second))
    held = jnp.concatenate(held)
    return jnp.concatenate([held, grid.take(held, 0, 0, 1)])


def scatter_sum(grid, terms):
    half = terms.shape[0] // grid.cores
    other = grid.give(terms[half:].astype(jnp.bfloat16), 0, 0, 1)
    pair = terms[:half] + other.astype(jnp.float32)
    rows = half // (grid.side * grid.side)
    total = pair[:rows]
    sent = pair.astype(jnp.bfloat16)
    for k in range(1, grid.side * grid.side):
        dy, dx = divmod(k, grid.side)
        total = total + grid.give(sent[k * rows : (k + 1) * rows], dy, dx, 0).astype(jnp.float32)
    return total


def chained_middle(grid, gathered, w_up, up_bias, w_down):
    n_row, tokens, units = grid.n_row, gathered.shape[0], w_up.shape[1]
    half = tokens // 2
    row = lax.axis_index("row")
    middle = n_row // 2
    upper = row >= middle
    depth = jnp.where(upper, n_row - 1 - row, row)
    inward = [(i, i + 1) for i in range(middle - 1)] + [(i, i - 1) for i in range(middle + 1, n_row)]
    outward = [(j, i) for i, j in inward]
    across = [(middle - 1, middle), (middle, middle - 1)]
    acc = jnp.dot(gathered, w_up, preferred_element_type=jnp.float32).astype(jnp.bfloat16)
    partial = acc.astype(jnp.float32)
    for _ in range(middle - 1):
        acc = (partial + lax.ppermute(acc, "row", inward).astype(jnp.float32)).astype(jnp.bfloat16)
    crossed = lax.ppermute(jnp.where(upper, acc[:half], acc[half:]), "row", across)
    summed = jnp.where(upper, acc[half:], acc[:half]).astype(jnp.float32) + crossed.astype(jnp.float32)
    own = jax.nn.gelu(summed + up_bias, approximate=True).astype(jnp.bfloat16)
    other = lax.ppermute(own, "row", across)
    out = jnp.where(upper, jnp.concatenate([other, own]), jnp.concatenate([own, other]))
    for hop in range(middle - 1):
        got = lax.ppermute(out, "row", outward)
        out = jnp.where(depth == middle - 2 - hop, got, out)
    return jnp.dot(out, w_down, preferred_element_type=jnp.float32)


def four_rows(grid, gathered, w_up, up_bias, w_down):
    tokens, units = gathered.shape[0], w_up.shape[1]
    half = tokens // 2
    row = lax.axis_index("row")
    upper = row >= 2
    is_end = jnp.logical_or(row == 0, row == 3)
    facing = [(0, 1), (1, 0), (2, 3), (3, 2)]
    outward = [(1, 0), (2, 3)]
    across = [(1, 2), (2, 1)]
    pieces = units // 128
    total = sum(SHARES)
    edges = [0]
    for share in SHARES:
        edges.append(edges[-1] + share)
    edges = [pieces * e // total * 128 for e in edges]
    count = len(SHARES)
    size = [edges[k + 1] - edges[k] for k in range(count)]

    def own_of(v):
        return jnp.where(upper, v[half:], v[:half])

    def other_of(v):
        return jnp.where(upper, v[:half], v[half:])

    def up(k):
        product = jnp.dot(gathered, w_up[:, edges[k] : edges[k + 1]], preferred_element_type=jnp.float32)
        return product.astype(jnp.bfloat16)

    def down(first, last, hidden):
        return jnp.dot(hidden, w_down[edges[first] : edges[last]], preferred_element_type=jnp.float32)

    def widened(v, width):
        return v if v.shape[1] == width else jnp.pad(v, ((0, 0), (0, width - v.shape[1])))

    partial = {0: up(0)}
    sums, own, other, got_own, hidden = {}, {}, {}, {}, {}
    terms, done = None, 0
    for t in range(count + 3):
        first, second = t - 2, t - 3
        faced = crossed = None
        has_own, has_other = 0 <= first < count, 0 <= second < count
        if t < count:
            sent = partial[t]
            if has_own:
                width = max(size[t], size[first], size[second] if has_other else 0)
                rows = [widened(own[first], width)]
                rows.append(widened(other[second], width) if has_other else rows[0])
                sent = jnp.where(is_end, widened(sent, width), jnp.concatenate(rows))
            faced = lax.ppermute(sent, "row", facing)
        elif has_own and has_other:
            faced = lax.ppermute(jnp.concatenate([own[first], other[second]], axis=1), "row", outward)
        elif has_other:
            faced = lax.ppermute(other[second], "row", outward)
        across_parts = []
        if 0 <= t - 1 < count:
            across_parts.append(other_of(sums[t - 1]))
        if has_own:
            across_parts.append(own[first])
        if across_parts:
            crossed = lax.ppermute(jnp.concatenate(across_parts, axis=1), "row", across)
        computed = []
        if t + 1 < count:
            partial[t + 1] = up(t + 1)
            computed.append(partial[t + 1])
        ready = t - 3
        if t >= count and ready > done:
            block = jnp.concatenate([hidden[k] for k in range(done, ready)], axis=1)
            product = down(done, ready, block)
            terms = product if terms is None else terms + product
            done = ready
            computed.append(terms)
        joined = lax.optimization_barrier(tuple(v for v in (faced, crossed, *computed) if v is not None))
        joined = list(joined)
        if faced is not None:
            faced = joined.pop(0)
        if crossed is not None:
            crossed = joined.pop(0)
        if t + 1 < count:
            partial[t + 1] = joined.pop(0)
        if joined:
            terms = joined.pop(0)
        if 0 <= t - 1 < count:
            k = t - 1
            summed = own_of(sums[k]).astype(jnp.float32) + crossed[:, : size[k]].astype(jnp.float32)
            summed = summed + up_bias[edges[k] : edges[k + 1]]
            own[k] = jax.nn.gelu(summed, approximate=True).astype(jnp.bfloat16)
        if has_own:
            other[first] = crossed[:, crossed.shape[1] - size[first] :]
        if t < count:
            came = faced[:, : size[t]].astype(jnp.float32)
            sums[t] = (partial[t].astype(jnp.float32) + came).astype(jnp.bfloat16)
            if has_own:
                got_own[first] = faced[:half, : size[first]]
            if has_other:
                got_other = faced[half:, : size[second]]
        else:
            if has_own:
                got_own[first] = faced[:, : size[first]]
            if has_other:
                got_other = faced[:, faced.shape[1] - size[second] :]
        if has_other:
            mine = jnp.where(is_end, got_own[second], own[second])
            theirs = jnp.where(is_end, got_other, other[second])
            lower = jnp.where(upper, theirs, mine)
            higher = jnp.where(upper, mine, theirs)
            hidden[second] = jnp.concatenate([lower, higher])
    block = jnp.concatenate([hidden[k] for k in range(done, count)], axis=1)
    product = down(done, count, block)
    return product if terms is None else terms + product


def local(grid, inputs, ln_gain, ln_bias, w_up, up_bias, w_down, down_bias):
    width = inputs.shape[1] * grid.n_row
    in_float = inputs.astype(jnp.float32)
    sums = jnp.stack([jnp.sum(in_float, axis=1), jnp.sum(in_float * in_float, axis=1)])
    total = row_sum(grid, sums)
    average = total[0] / width
    variance = total[1] / width - average * average
    normed = (in_float - average[:, None]) * lax.rsqrt(variance + 1e-05)[:, None]
    normed = (normed * ln_gain + ln_bias).astype(jnp.bfloat16)
    gathered = gather(grid, normed)
    block = four_rows if grid.n_row == 4 else chained_middle
    terms = block(grid, gathered, w_up, up_bias, w_down)
    down_sum = scatter_sum(grid, terms)
    return (in_float + down_sum + down_bias).astype(jnp.bfloat16)


def solution(mesh):
    grid = Grid(mesh.shape["row"], mesh.shape["col"])
    placed = (
        P("col", "row"),
        P("row"),
        P("row"),
        P("row", "col"),
        P("col"),
        P("col", "row"),
        P("row"),
    )
    return jax.shard_map(
        functools.partial(local, grid), mesh=mesh, in_specs=placed, out_specs=P("col", "row"), check_vma=False
    )
```

```python
import functools
import math

import jax
import jax.numpy as jnp
from jax import lax
from jax.sharding import PartitionSpec as P


SHARES = (3, 3, 3, 3, 3, 3, 3, 3)
UP_AHEAD = 3
DOWN_AHEAD = 2


class Grid:
    def __init__(self, n_row, n_col):
        self.n_row, self.n_col = n_row, n_col
        self.cores = 2
        self.side = math.isqrt(n_col // self.cores)

    def shifted(self, index, dy, dx, dc):
        y, rest = divmod(index, self.side * self.cores)
        x, core = divmod(rest, self.cores)
        y, x = (y + dy) % self.side, (x + dx) % self.side
        core = (core + dc) % self.cores
        return (y * self.side + x) * self.cores + core

    def take(self, value, dy, dx, dc):
        pairs = [(self.shifted(i, dy, dx, dc), i) for i in range(self.n_col)]
        return lax.ppermute(value, "col", pairs)

    def give(self, value, dy, dx, dc):
        pairs = [(i, self.shifted(i, dy, dx, dc)) for i in range(self.n_col)]
        return lax.ppermute(value, "col", pairs)

    def turn(self, value, step):
        pairs = []
        for i in range(self.n_col):
            far = (step, 0, 0) if i % self.cores == 0 else (0, step, 0)
            pairs.append((self.shifted(i, *far), i))
        return lax.ppermute(value, "col", pairs)


def row_sum(grid, value):
    total = value
    for step in range(1, grid.n_row):
        pairs = [(i, (i + step) % grid.n_row) for i in range(grid.n_row)]
        total = total + lax.ppermute(value, "row", pairs)
    return total


def gather(grid, own):
    side = grid.side
    core = lax.axis_index("col") % grid.cores
    along_x = [grid.take(own, 0, d, 0) for d in range(1, side)]
    along_y = [grid.take(own, d, 0, 0) for d in range(1, side)]
    turned = jnp.where(core == 0, jnp.concatenate(along_x), jnp.concatenate(along_y))
    rows = own.shape[0]
    far = {}
    for step in range(1, side):
        block = grid.turn(turned, step)
        for d in range(1, side):
            far[step, d] = block[(d - 1) * rows : d * rows]
    held = []
    for dy in range(side):
        for dx in range(side):
            if dy == 0 and dx == 0:
                held.append(own)
            elif dy == 0:
                held.append(along_x[dx - 1])
            elif dx == 0:
                held.append(along_y[dy - 1])
            else:
                first, second = far[dy, dx], far[dx, dy]
                held.append(first if side == 2 else jnp.where(core == 0, first, second))
    held = jnp.concatenate(held)
    return jnp.concatenate([held, grid.take(held, 0, 0, 1)])


def scatter_sum(grid, terms):
    half = terms.shape[0] // grid.cores
    other = grid.give(terms[half:].astype(jnp.bfloat16), 0, 0, 1)
    pair = terms[:half] + other.astype(jnp.float32)
    rows = half // (grid.side * grid.side)
    total = pair[:rows]
    sent = pair.astype(jnp.bfloat16)
    for k in range(1, grid.side * grid.side):
        dy, dx = divmod(k, grid.side)
        total = total + grid.give(sent[k * rows : (k + 1) * rows], dy, dx, 0).astype(jnp.float32)
    return total


def chained_middle(grid, early, gathered, w_up, up_bias, w_down):
    n_row, tokens = grid.n_row, gathered.shape[0]
    half = tokens // 2
    row = lax.axis_index("row")
    middle = n_row // 2
    upper = row >= middle
    depth = jnp.where(upper, n_row - 1 - row, row)
    inward = [(i, i + 1) for i in range(middle - 1)] + [(i, i - 1) for i in range(middle + 1, n_row)]
    outward = [(j, i) for i, j in inward]
    across = [(middle - 1, middle), (middle, middle - 1)]
    acc = jnp.dot(gathered, w_up, preferred_element_type=jnp.float32).astype(jnp.bfloat16)
    partial = acc.astype(jnp.float32)
    for _ in range(middle - 1):
        acc = (partial + lax.ppermute(acc, "row", inward).astype(jnp.float32)).astype(jnp.bfloat16)
    crossed = lax.ppermute(jnp.where(upper, acc[:half], acc[half:]), "row", across)
    summed = jnp.where(upper, acc[half:], acc[:half]).astype(jnp.float32) + crossed.astype(jnp.float32)
    own = jax.nn.gelu(summed + up_bias, approximate=True).astype(jnp.bfloat16)
    other = lax.ppermute(own, "row", across)
    out = jnp.where(upper, jnp.concatenate([other, own]), jnp.concatenate([own, other]))
    for hop in range(middle - 1):
        got = lax.ppermute(out, "row", outward)
        out = jnp.where(depth == middle - 2 - hop, got, out)
    return jnp.dot(out, w_down, preferred_element_type=jnp.float32)


def chunk_edges(units):
    pieces, edges = units // 128, [0]
    for share in SHARES:
        edges.append(edges[-1] + share)
    return [pieces * e // edges[-1] * 128 for e in edges]


def cut(weights, axis, low, high, after):
    weights, _ = lax.optimization_barrier((weights, after))
    return lax.optimization_barrier(lax.slice_in_dim(weights, low, high, axis=axis))


def four_rows(grid, early, gathered, w_up, up_bias, w_down):
    row = lax.axis_index("row")
    is_end = jnp.logical_or(row == 0, row == 3)
    facing = [(0, 1), (1, 0), (2, 3), (3, 2)]
    outward = [(1, 0), (2, 3)]
    across = []
    for i in range(grid.n_row * grid.n_col):
        own_row, own_col = divmod(i, grid.n_col)
        if own_row in (1, 2):
            across.append((i, (3 - own_row) * grid.n_col + own_col))
        else:
            across.append((i, own_row * grid.n_col + grid.shifted(own_col, 0, 0, 1)))
    edges = chunk_edges(w_up.shape[1])
    count = len(SHARES)
    size = [edges[k + 1] - edges[k] for k in range(count)]

    def face(sent, pairs):
        return lax.ppermute(sent, "row", pairs)

    def cross(sent):
        return lax.ppermute(sent, ("row", "col"), across)

    up_part, down_part = dict(enumerate(early)), {}

    def stage(t, after):
        k = t + UP_AHEAD
        if k < count and k not in up_part:
            up_part[k] = cut(w_up, 1, edges[k], edges[k + 1], after)
        k = t - 3 + DOWN_AHEAD
        if 0 <= k < count:
            down_part[k] = cut(w_down, 0, edges[k], edges[k + 1], after)

    def up(k):
        return jnp.dot(gathered, up_part[k], preferred_element_type=jnp.float32).astype(jnp.bfloat16)

    def down(k):
        return jnp.dot(hidden[k], down_part[k], preferred_element_type=jnp.float32)

    def widened(v, width):
        return v if v.shape[1] == width else jnp.pad(v, ((0, 0), (0, width - v.shape[1])))

    for k in range(len(early), UP_AHEAD):
        up_part[k] = cut(w_up, 1, edges[k], edges[k + 1], gathered)
    partial, sums, own, hidden = {0: up(0)}, {}, {}, {}
    terms = None
    for t in range(count + 2):
        crossed = None
        if t < 2:
            faced = face(partial[t], facing)
        elif t < count:
            width = max(size[t], size[t - 2])
            faced = face(jnp.where(is_end, widened(partial[t], width), widened(own[t - 2], width)), facing)
        else:
            faced = face(own[t - 2], outward)
        if 0 <= t - 1 < count:
            crossed = cross(sums[t - 1])
        stage(t, partial[t] if t < count else terms)
        computed = []
        if t + 1 < count:
            partial[t + 1] = up(t + 1)
            computed.append(partial[t + 1])
        if t >= 3:
            product = down(t - 3)
            terms = product if terms is None else terms + product
            computed.append(terms)
        joined = list(lax.optimization_barrier(tuple(v for v in (faced, crossed, *computed) if v is not None)))
        faced = joined.pop(0)
        if crossed is not None:
            crossed = joined.pop(0)
        if t + 1 < count:
            partial[t + 1] = joined.pop(0)
        if joined:
            terms = joined.pop(0)
        if crossed is not None:
            k = t - 1
            summed = sums[k].astype(jnp.float32) + crossed.astype(jnp.float32)
            summed = summed + up_bias[edges[k] : edges[k + 1]]
            own[k] = jax.nn.gelu(summed, approximate=True).astype(jnp.bfloat16)
        if t < count:
            sums[t] = (partial[t].astype(jnp.float32) + faced[:, : size[t]].astype(jnp.float32)).astype(jnp.bfloat16)
        if t >= 2:
            hidden[t - 2] = jnp.where(is_end, faced[:, : size[t - 2]], own[t - 2])
    return terms + down(count - 1)


def local(grid, inputs, ln_gain, ln_bias, w_up, up_bias, w_down, down_bias):
    width = inputs.shape[1] * grid.n_row
    place = (lax.axis_index("row"), lax.axis_index("col"))
    early = []
    if grid.n_row == 4:
        edges = chunk_edges(w_up.shape[1])
        early.append(cut(w_up, 1, edges[0], edges[1], place))
    in_float = inputs.astype(jnp.float32)
    sums = jnp.stack([jnp.sum(in_float, axis=1), jnp.sum(in_float * in_float, axis=1)])
    total = row_sum(grid, sums)
    average = total[0] / width
    variance = total[1] / width - average * average
    normed = (in_float - average[:, None]) * lax.rsqrt(variance + 1e-05)[:, None]
    normed = (normed * ln_gain + ln_bias).astype(jnp.bfloat16)
    if grid.n_row == 4:
        early.append(cut(w_up, 1, edges[1], edges[2], normed))
    gathered = gather(grid, normed)
    block = four_rows if grid.n_row == 4 else chained_middle
    terms = block(grid, early, gathered, w_up, up_bias, w_down)
    down_sum = scatter_sum(grid, terms)
    return (in_float + down_sum + down_bias).astype(jnp.bfloat16)


def solution(mesh):
    grid = Grid(mesh.shape["row"], mesh.shape["col"])
    placed = (
        P("col", "row"),
        P("row"),
        P("row"),
        P("row", "col"),
        P("col"),
        P("col", "row"),
        P("row"),
    )
    return jax.shard_map(
        functools.partial(local, grid), mesh=mesh, in_specs=placed, out_specs=P("col", "row"), check_vma=False
    )
```

```python
import functools
import math

import jax
import jax.numpy as jnp
from jax import lax
from jax.sharding import PartitionSpec as P


SHARES = (3, 3, 3, 3, 3, 3, 3, 3)
UP_AHEAD = 3
DOWN_AHEAD = 2


class Grid:
    def __init__(self, n_row, n_col):
        self.n_row, self.n_col = n_row, n_col
        self.cores = 2
        self.side = math.isqrt(n_col // self.cores)

    def shifted(self, index, dy, dx, dc):
        y, rest = divmod(index, self.side * self.cores)
        x, core = divmod(rest, self.cores)
        y, x = (y + dy) % self.side, (x + dx) % self.side
        core = (core + dc) % self.cores
        return (y * self.side + x) * self.cores + core

    def take(self, value, dy, dx, dc):
        pairs = [(self.shifted(i, dy, dx, dc), i) for i in range(self.n_col)]
        return lax.ppermute(value, "col", pairs)

    def give(self, value, dy, dx, dc):
        pairs = [(i, self.shifted(i, dy, dx, dc)) for i in range(self.n_col)]
        return lax.ppermute(value, "col", pairs)


def row_sum(grid, value):
    step = 1
    while step < grid.n_row:
        value = value + lax.ppermute(value, "row", [(i, i ^ step) for i in range(grid.n_row)])
        step *= 2
    return value


def gather(grid, own):
    held = [own]
    for k in range(1, grid.side * grid.side):
        held.append(grid.take(own, k // grid.side, k % grid.side, 0))
    held = jnp.concatenate(held)
    return jnp.concatenate([held, grid.take(held, 0, 0, 1)])


def scatter_sum(grid, terms):
    half = terms.shape[0] // grid.cores
    other = grid.give(terms[half:].astype(jnp.bfloat16), 0, 0, 1)
    pair = terms[:half] + other.astype(jnp.float32)
    rows = half // (grid.side * grid.side)
    total = pair[:rows]
    sent = pair.astype(jnp.bfloat16)
    for k in range(1, grid.side * grid.side):
        dy, dx = divmod(k, grid.side)
        total = total + grid.give(sent[k * rows : (k + 1) * rows], dy, dx, 0).astype(jnp.float32)
    return total


def chained_middle(grid, gathered, w_up, up_bias, w_down):
    n_row, tokens = grid.n_row, gathered.shape[0]
    half = tokens // 2
    row = lax.axis_index("row")
    middle = n_row // 2
    upper = row >= middle
    depth = jnp.where(upper, n_row - 1 - row, row)
    inward = [(i, i + 1) for i in range(middle - 1)] + [(i, i - 1) for i in range(middle + 1, n_row)]
    outward = [(j, i) for i, j in inward]
    across = [(middle - 1, middle), (middle, middle - 1)]
    acc = jnp.dot(gathered, w_up, preferred_element_type=jnp.float32).astype(jnp.bfloat16)
    partial = acc.astype(jnp.float32)
    for _ in range(middle - 1):
        acc = (partial + lax.ppermute(acc, "row", inward).astype(jnp.float32)).astype(jnp.bfloat16)
    crossed = lax.ppermute(jnp.where(upper, acc[:half], acc[half:]), "row", across)
    summed = jnp.where(upper, acc[half:], acc[:half]).astype(jnp.float32) + crossed.astype(jnp.float32)
    own = jax.nn.gelu(summed + up_bias, approximate=True).astype(jnp.bfloat16)
    other = lax.ppermute(own, "row", across)
    out = jnp.where(upper, jnp.concatenate([other, own]), jnp.concatenate([own, other]))
    for hop in range(middle - 1):
        got = lax.ppermute(out, "row", outward)
        out = jnp.where(depth == middle - 2 - hop, got, out)
    return jnp.dot(out, w_down, preferred_element_type=jnp.float32)


def chunk_edges(units):
    pieces, edges = units // 128, [0]
    for share in SHARES:
        edges.append(edges[-1] + share)
    return [pieces * e // edges[-1] * 128 for e in edges]


def cut(weights, axis, low, high, after):
    weights, _ = lax.optimization_barrier((weights, after))
    return lax.optimization_barrier(lax.slice_in_dim(weights, low, high, axis=axis))


def four_rows(grid, is_end, early, gathered, w_up, up_bias, w_down):
    facing = [(0, 1), (1, 0), (2, 3), (3, 2)]
    across = []
    for i in range(grid.n_row * grid.n_col):
        own_row, own_col = divmod(i, grid.n_col)
        if own_row in (1, 2):
            across.append((i, (3 - own_row) * grid.n_col + own_col))
        else:
            across.append((i, own_row * grid.n_col + grid.shifted(own_col, 0, 0, 1)))
    edges = chunk_edges(w_up.shape[1])
    count = len(SHARES)
    size = [edges[k + 1] - edges[k] for k in range(count)]

    def face(sent, pairs):
        return lax.ppermute(sent, "row", pairs)

    def cross(sent):
        return lax.ppermute(sent, ("row", "col"), across)

    up_part, down_part = dict(enumerate(early)), {}

    def stage(t, after):
        k = t + UP_AHEAD
        if k < count and k not in up_part:
            up_part[k] = cut(w_up, 1, edges[k], edges[k + 1], after)
        k = t - 3 + DOWN_AHEAD
        if 0 <= k < count:
            down_part[k] = cut(w_down, 0, edges[k], edges[k + 1], after)

    def up(k):
        return jnp.dot(gathered, up_part[k], preferred_element_type=jnp.float32).astype(jnp.bfloat16)

    def down(k):
        return jnp.dot(hidden[k], down_part[k], preferred_element_type=jnp.float32)

    def widened(v, width):
        return v if v.shape[1] == width else jnp.pad(v, ((0, 0), (0, width - v.shape[1])))

    for k in range(len(early), UP_AHEAD):
        up_part[k] = cut(w_up, 1, edges[k], edges[k + 1], gathered)
    partial, sums, own, hidden = {0: up(0)}, {}, {}, {}
    terms = None
    for t in range(count + 2):
        crossed = None
        if t < 2:
            faced = face(partial[t], facing)
        elif t < count:
            width = max(size[t], size[t - 2])
            faced = face(jnp.where(is_end, widened(partial[t], width), widened(own[t - 2], width)), facing)
        else:
            faced = face(own[t - 2], facing)
        if 0 <= t - 1 < count:
            crossed = cross(sums[t - 1])
        stage(t, partial[t] if t < count else terms)
        computed = []
        if t + 1 < count:
            partial[t + 1] = up(t + 1)
            computed.append(partial[t + 1])
        if t >= 3:
            product = down(t - 3)
            terms = product if terms is None else terms + product
            computed.append(terms)
        joined = list(lax.optimization_barrier(tuple(v for v in (faced, crossed, *computed) if v is not None)))
        faced = joined.pop(0)
        if crossed is not None:
            crossed = joined.pop(0)
        if t + 1 < count:
            partial[t + 1] = joined.pop(0)
        if joined:
            terms = joined.pop(0)
        if crossed is not None:
            k = t - 1
            summed = sums[k].astype(jnp.float32) + crossed.astype(jnp.float32)
            summed = summed + up_bias[edges[k] : edges[k + 1]]
            own[k] = jax.nn.gelu(summed, approximate=True).astype(jnp.bfloat16)
        if t < count:
            sums[t] = (partial[t].astype(jnp.float32) + faced[:, : size[t]].astype(jnp.float32)).astype(jnp.bfloat16)
        if t >= 2:
            hidden[t - 2] = jnp.where(is_end, faced[:, : size[t - 2]], own[t - 2])
    return terms + down(count - 1)


def local(grid, inputs, ln_gain, ln_bias, w_up, up_bias, w_down, down_bias):
    width = inputs.shape[1] * grid.n_row
    early = []
    if grid.n_row == 4:
        row = lax.axis_index("row")
        is_end, w_first = lax.optimization_barrier((jnp.logical_or(row == 0, row == 3), w_up))
        edges = chunk_edges(w_up.shape[1])
        early.append(lax.optimization_barrier(lax.slice_in_dim(w_first, edges[0], edges[1], axis=1)))
    in_float = inputs.astype(jnp.float32)
    sums = jnp.stack([jnp.sum(in_float, axis=1), jnp.sum(in_float * in_float, axis=1)])
    total = row_sum(grid, sums)
    average = total[0] / width
    variance = total[1] / width - average * average
    normed = (in_float - average[:, None]) * lax.rsqrt(variance + 1e-05)[:, None]
    normed = (normed * ln_gain + ln_bias).astype(jnp.bfloat16)
    if grid.n_row == 4:
        early.append(cut(w_up, 1, edges[1], edges[2], normed))
    gathered = gather(grid, normed)
    if grid.n_row == 4:
        terms = four_rows(grid, is_end, early, gathered, w_up, up_bias, w_down)
    else:
        terms = chained_middle(grid, gathered, w_up, up_bias, w_down)
    down_sum = scatter_sum(grid, terms)
    return (in_float + down_sum + down_bias).astype(jnp.bfloat16)


def solution(mesh):
    grid = Grid(mesh.shape["row"], mesh.shape["col"])
    placed = (
        P("col", "row"),
        P("row"),
        P("row"),
        P("row", "col"),
        P("col"),
        P("col", "row"),
        P("row"),
    )
    return jax.shard_map(
        functools.partial(local, grid), mesh=mesh, in_specs=placed, out_specs=P("col", "row"), check_vma=False
    )
```

```python
import functools
import math

import jax
import jax.numpy as jnp
from jax import lax
from jax.sharding import PartitionSpec as P


SHARES = (3, 3, 3, 3, 3, 3, 3, 3)
UP_AHEAD = 3
DOWN_AHEAD = 3


class Grid:
    def __init__(self, n_row, n_col):
        self.n_row, self.n_col = n_row, n_col
        self.cores = 2
        self.side = math.isqrt(n_col // self.cores)

    def shifted(self, index, dy, dx, dc):
        y, rest = divmod(index, self.side * self.cores)
        x, core = divmod(rest, self.cores)
        y, x = (y + dy) % self.side, (x + dx) % self.side
        core = (core + dc) % self.cores
        return (y * self.side + x) * self.cores + core

    def take(self, value, dy, dx, dc):
        pairs = [(self.shifted(i, dy, dx, dc), i) for i in range(self.n_col)]
        return lax.ppermute(value, "col", pairs)

    def give(self, value, dy, dx, dc):
        pairs = [(i, self.shifted(i, dy, dx, dc)) for i in range(self.n_col)]
        return lax.ppermute(value, "col", pairs)


def row_sum(grid, value):
    step = 1
    while step < grid.n_row:
        value = value + lax.ppermute(value, "row", [(i, i ^ step) for i in range(grid.n_row)])
        step *= 2
    return value


def gather(grid, own):
    held = [own]
    for k in range(1, grid.side * grid.side):
        held.append(grid.take(own, k // grid.side, k % grid.side, 0))
    held = jnp.concatenate(held)
    return held, grid.take(held, 0, 0, 1)


def scatter_sum(grid, kept, given):
    half = kept.shape[0]
    other = grid.give(given.astype(jnp.bfloat16), 0, 0, 1)
    pair = kept + other.astype(jnp.float32)
    rows = half // (grid.side * grid.side)
    total = pair[:rows]
    sent = pair.astype(jnp.bfloat16)
    for k in range(1, grid.side * grid.side):
        dy, dx = divmod(k, grid.side)
        total = total + grid.give(sent[k * rows : (k + 1) * rows], dy, dx, 0).astype(jnp.float32)
    return total


def chained_middle(grid, held, swapped, w_up, up_bias, w_down):
    n_row = grid.n_row
    gathered = jnp.concatenate([held, swapped])
    half = held.shape[0]
    row = lax.axis_index("row")
    middle = n_row // 2
    upper = row >= middle
    depth = jnp.where(upper, n_row - 1 - row, row)
    inward = [(i, i + 1) for i in range(middle - 1)] + [(i, i - 1) for i in range(middle + 1, n_row)]
    outward = [(j, i) for i, j in inward]
    across = [(middle - 1, middle), (middle, middle - 1)]
    acc = jnp.dot(gathered, w_up, preferred_element_type=jnp.float32).astype(jnp.bfloat16)
    partial = acc.astype(jnp.float32)
    for _ in range(middle - 1):
        acc = (partial + lax.ppermute(acc, "row", inward).astype(jnp.float32)).astype(jnp.bfloat16)
    crossed = lax.ppermute(jnp.where(upper, acc[:half], acc[half:]), "row", across)
    summed = jnp.where(upper, acc[half:], acc[:half]).astype(jnp.float32) + crossed.astype(jnp.float32)
    own = jax.nn.gelu(summed + up_bias, approximate=True).astype(jnp.bfloat16)
    other = lax.ppermute(own, "row", across)
    out = jnp.where(upper, jnp.concatenate([other, own]), jnp.concatenate([own, other]))
    for hop in range(middle - 1):
        got = lax.ppermute(out, "row", outward)
        out = jnp.where(depth == middle - 2 - hop, got, out)
    terms = jnp.dot(out, w_down, preferred_element_type=jnp.float32)
    return terms[:half], terms[half:]


def chunk_edges(units):
    pieces, edges = units // 128, [0]
    for share in SHARES:
        edges.append(edges[-1] + share)
    return [pieces * e // edges[-1] * 128 for e in edges]


def cut(weights, axis, low, high, after):
    weights, _ = lax.optimization_barrier((weights, after))
    return lax.optimization_barrier(lax.slice_in_dim(weights, low, high, axis=axis))


def four_rows(grid, is_end, early, held, swapped, w_up, up_bias, w_down):
    facing = [(0, 1), (1, 0), (2, 3), (3, 2)]
    across = []
    for i in range(grid.n_row * grid.n_col):
        own_row, own_col = divmod(i, grid.n_col)
        if own_row in (1, 2):
            across.append((i, (3 - own_row) * grid.n_col + own_col))
        else:
            across.append((i, own_row * grid.n_col + grid.shifted(own_col, 0, 0, 1)))
    edges = chunk_edges(w_up.shape[1])
    count = len(SHARES)
    size = [edges[k + 1] - edges[k] for k in range(count)]

    def face(sent, pairs):
        return lax.ppermute(sent, "row", pairs)

    def cross(sent):
        return lax.ppermute(sent, ("row", "col"), across)

    up_part, down_part = dict(enumerate(early)), {}

    def stage(t, after):
        k = t + UP_AHEAD
        if k < count and k not in up_part:
            up_part[k] = cut(w_up, 1, edges[k], edges[k + 1], after)
        k = t - 3 + DOWN_AHEAD
        if 0 <= k < count:
            down_part[k] = cut(w_down, 0, edges[k], edges[k + 1], after)
        if k == count - 1:
            down_part[count] = cut(w_down, 0, edges[k], edges[k + 1], down_part[k])

    def up(k):
        return jnp.dot(gathered, up_part[k], preferred_element_type=jnp.float32).astype(jnp.bfloat16)

    def down(k):
        return jnp.dot(hidden[k], down_part[k], preferred_element_type=jnp.float32)

    def widened(v, width):
        return v if v.shape[1] == width else jnp.pad(v, ((0, 0), (0, width - v.shape[1])))

    gathered, half = jnp.concatenate([held, swapped]), held.shape[0]
    for k in range(len(early), UP_AHEAD):
        up_part[k] = cut(w_up, 1, edges[k], edges[k + 1], gathered)
    first = [jnp.dot(v, up_part[0], preferred_element_type=jnp.float32).astype(jnp.bfloat16) for v in (held, swapped)]
    partial, sums, own, hidden = {0: jnp.concatenate(first)}, {}, {}, {}
    terms = None
    for t in range(count + 1):
        crossed = None
        if t == 0:
            faced = jnp.concatenate([face(v, facing) for v in first])
        elif t == 1:
            faced = face(partial[t], facing)
        elif t < count:
            width = max(size[t], size[t - 2])
            faced = face(jnp.where(is_end, widened(partial[t], width), widened(own[t - 2], width)), facing)
        else:
            faced = face(own[t - 2], facing)
        if 0 <= t - 1 < count:
            crossed = cross(sums[t - 1])
        stage(t, partial[t] if t < count else terms)
        computed = []
        if t + 1 < count:
            partial[t + 1] = up(t + 1)
            computed.append(partial[t + 1])
        if t >= 3:
            product = down(t - 3)
            terms = product if terms is None else terms + product
            computed.append(terms)
        joined = list(lax.optimization_barrier(tuple(v for v in (faced, crossed, *computed) if v is not None)))
        faced = joined.pop(0)
        if crossed is not None:
            crossed = joined.pop(0)
        if t + 1 < count:
            partial[t + 1] = joined.pop(0)
        if joined:
            terms = joined.pop(0)
        if crossed is not None:
            k = t - 1
            summed = sums[k].astype(jnp.float32) + crossed.astype(jnp.float32)
            summed = summed + up_bias[edges[k] : edges[k + 1]]
            own[k] = jax.nn.gelu(summed, approximate=True).astype(jnp.bfloat16)
        if t < count:
            sums[t] = (partial[t].astype(jnp.float32) + faced[:, : size[t]].astype(jnp.float32)).astype(jnp.bfloat16)
        if t >= 2:
            hidden[t - 2] = jnp.where(is_end, faced[:, : size[t - 2]], own[t - 2])
    last = own[count - 1]
    given = face(last[half:], facing)
    kept = face(last[:half], facing)
    terms = terms + down(count - 2)

    def finish(came, mine, before, weights):
        rows = jnp.where(is_end, came, mine)
        return before + jnp.dot(rows, weights, preferred_element_type=jnp.float32)

    given = finish(given, last[half:], terms[half:], down_part[count - 1])
    return finish(kept, last[:half], terms[:half], down_part[count]), given


def local(grid, inputs, ln_gain, ln_bias, w_up, up_bias, w_down, down_bias):
    width = inputs.shape[1] * grid.n_row
    early = []
    if grid.n_row == 4:
        row = lax.axis_index("row")
        is_end, w_first = lax.optimization_barrier((jnp.logical_or(row == 0, row == 3), w_up))
        edges = chunk_edges(w_up.shape[1])
        early.append(lax.optimization_barrier(lax.slice_in_dim(w_first, edges[0], edges[1], axis=1)))
    in_float = inputs.astype(jnp.float32)
    sums = jnp.stack([jnp.sum(in_float, axis=1), jnp.sum(in_float * in_float, axis=1)])
    total = row_sum(grid, sums)
    average = total[0] / width
    variance = total[1] / width - average * average
    normed = (in_float - average[:, None]) * lax.rsqrt(variance + 1e-05)[:, None]
    normed = (normed * ln_gain + ln_bias).astype(jnp.bfloat16)
    if grid.n_row == 4:
        early.append(cut(w_up, 1, edges[1], edges[2], normed))
    held, swapped = gather(grid, normed)
    if grid.n_row == 4:
        terms = four_rows(grid, is_end, early, held, swapped, w_up, up_bias, w_down)
    else:
        terms = chained_middle(grid, held, swapped, w_up, up_bias, w_down)
    down_sum = scatter_sum(grid, *terms)
    return (in_float + down_sum + down_bias).astype(jnp.bfloat16)


def solution(mesh):
    grid = Grid(mesh.shape["row"], mesh.shape["col"])
    placed = (
        P("col", "row"),
        P("row"),
        P("row"),
        P("row", "col"),
        P("col"),
        P("col", "row"),
        P("row"),
    )
    return jax.shard_map(
        functools.partial(local, grid), mesh=mesh, in_specs=placed, out_specs=P("col", "row"), check_vma=False
    )
```

```python
import functools
import math

import jax
import jax.numpy as jnp
from jax import lax
from jax.sharding import PartitionSpec as P


SHARES = (3, 3, 3, 3, 3, 3, 3, 3)
UP_AHEAD = 3
DOWN_AHEAD = 3


class Grid:
    def __init__(self, n_row, n_col):
        self.n_row, self.n_col = n_row, n_col
        self.cores = 2
        self.side = math.isqrt(n_col // self.cores)

    def shifted(self, index, dy, dx, dc):
        y, rest = divmod(index, self.side * self.cores)
        x, core = divmod(rest, self.cores)
        y, x = (y + dy) % self.side, (x + dx) % self.side
        core = (core + dc) % self.cores
        return (y * self.side + x) * self.cores + core

    def take(self, value, dy, dx, dc):
        pairs = [(self.shifted(i, dy, dx, dc), i) for i in range(self.n_col)]
        return lax.ppermute(value, "col", pairs)

    def give(self, value, dy, dx, dc):
        pairs = [(i, self.shifted(i, dy, dx, dc)) for i in range(self.n_col)]
        return lax.ppermute(value, "col", pairs)


def row_sum(grid, value):
    step = 1
    while step < grid.n_row:
        value = value + lax.ppermute(value, "row", [(i, i ^ step) for i in range(grid.n_row)])
        step *= 2
    return value


def gather(grid, own):
    held = [own]
    for k in range(1, grid.side * grid.side):
        held.append(grid.take(own, k // grid.side, k % grid.side, 0))
    return jnp.concatenate(held[:-1]), held[-1]


def scatter_sum(grid, kept, given):
    half = kept.shape[0]
    other = grid.give(given.astype(jnp.bfloat16), 0, 0, 1)
    pair = kept + other.astype(jnp.float32)
    rows = half // (grid.side * grid.side)
    total = pair[:rows]
    sent = pair.astype(jnp.bfloat16)
    for k in range(1, grid.side * grid.side):
        dy, dx = divmod(k, grid.side)
        total = total + grid.give(sent[k * rows : (k + 1) * rows], dy, dx, 0).astype(jnp.float32)
    return total


def chained_middle(grid, sooner, farthest, w_up, up_bias, w_down):
    n_row = grid.n_row
    held = jnp.concatenate([sooner, farthest])
    gathered = jnp.concatenate([held, grid.take(held, 0, 0, 1)])
    half = held.shape[0]
    row = lax.axis_index("row")
    middle = n_row // 2
    upper = row >= middle
    depth = jnp.where(upper, n_row - 1 - row, row)
    inward = [(i, i + 1) for i in range(middle - 1)] + [(i, i - 1) for i in range(middle + 1, n_row)]
    outward = [(j, i) for i, j in inward]
    across = [(middle - 1, middle), (middle, middle - 1)]
    acc = jnp.dot(gathered, w_up, preferred_element_type=jnp.float32).astype(jnp.bfloat16)
    partial = acc.astype(jnp.float32)
    for _ in range(middle - 1):
        acc = (partial + lax.ppermute(acc, "row", inward).astype(jnp.float32)).astype(jnp.bfloat16)
    crossed = lax.ppermute(jnp.where(upper, acc[:half], acc[half:]), "row", across)
    summed = jnp.where(upper, acc[half:], acc[:half]).astype(jnp.float32) + crossed.astype(jnp.float32)
    own = jax.nn.gelu(summed + up_bias, approximate=True).astype(jnp.bfloat16)
    other = lax.ppermute(own, "row", across)
    out = jnp.where(upper, jnp.concatenate([other, own]), jnp.concatenate([own, other]))
    for hop in range(middle - 1):
        got = lax.ppermute(out, "row", outward)
        out = jnp.where(depth == middle - 2 - hop, got, out)
    terms = jnp.dot(out, w_down, preferred_element_type=jnp.float32)
    return terms[:half], terms[half:]


def chunk_edges(units):
    pieces, edges = units // 128, [0]
    for share in SHARES:
        edges.append(edges[-1] + share)
    return [pieces * e // edges[-1] * 128 for e in edges]


def cut(weights, axis, low, high, after):
    weights, _ = lax.optimization_barrier((weights, after))
    return lax.optimization_barrier(lax.slice_in_dim(weights, low, high, axis=axis))


def four_rows(grid, is_end, early, sooner, farthest, w_up, up_bias, w_down):
    facing = [(0, 1), (1, 0), (2, 3), (3, 2)]
    across = []
    for i in range(grid.n_row * grid.n_col):
        own_row, own_col = divmod(i, grid.n_col)
        if own_row in (1, 2):
            across.append((i, (3 - own_row) * grid.n_col + own_col))
        else:
            across.append((i, own_row * grid.n_col + grid.shifted(own_col, 0, 0, 1)))
    edges = chunk_edges(w_up.shape[1])
    count = len(SHARES)
    size = [edges[k + 1] - edges[k] for k in range(count)]

    def face(sent, pairs):
        return lax.ppermute(sent, "row", pairs)

    def cross(sent):
        return lax.ppermute(sent, ("row", "col"), across)

    up_part, down_part = dict(enumerate(early)), {}

    def stage(t, after):
        k = t + UP_AHEAD
        if k < count and k not in up_part:
            up_part[k] = cut(w_up, 1, edges[k], edges[k + 1], after)
        k = t - 3 + DOWN_AHEAD
        if 0 <= k < count:
            down_part[k] = cut(w_down, 0, edges[k], edges[k + 1], after)
        if k == count - 1:
            down_part[count] = cut(w_down, 0, edges[k], edges[k + 1], down_part[k])

    def up(k):
        return jnp.dot(gathered, up_part[k], preferred_element_type=jnp.float32).astype(jnp.bfloat16)

    def down(k):
        return jnp.dot(hidden[k], down_part[k], preferred_element_type=jnp.float32)

    def activated(k, mine, came):
        summed = mine.astype(jnp.float32) + came.astype(jnp.float32) + up_bias[edges[k] : edges[k + 1]]
        return jax.nn.gelu(summed, approximate=True).astype(jnp.bfloat16)

    def widened(v, width):
        return v if v.shape[1] == width else jnp.pad(v, ((0, 0), (0, width - v.shape[1])))

    def up_first(v):
        return jnp.dot(v, up_part[0], preferred_element_type=jnp.float32).astype(jnp.bfloat16)

    first = [up_first(sooner)]
    farthest, first[0] = lax.optimization_barrier((farthest, first[0]))
    held = jnp.concatenate([sooner, farthest])
    half = held.shape[0]
    later = jnp.concatenate([farthest, grid.take(held, 0, 0, 1)])
    gathered = jnp.concatenate([sooner, later])
    first.append(up_first(later))
    for k in range(len(early), UP_AHEAD):
        up_part[k] = cut(w_up, 1, edges[k], edges[k + 1], gathered)
    partial, sums, own, hidden = {0: jnp.concatenate(first)}, {}, {}, {}
    terms = None
    for t in range(count):
        crossed = None
        if t == 0:
            faced = jnp.concatenate([face(v, facing) for v in first])
        elif t == 1:
            faced = face(partial[t], facing)
        elif t < count:
            width = max(size[t], size[t - 2])
            faced = face(jnp.where(is_end, widened(partial[t], width), widened(own[t - 2], width)), facing)
        if t > 0:
            crossed = cross(sums[t - 1])
        stage(t, partial[t])
        computed = []
        if t + 1 < count:
            partial[t + 1] = up(t + 1)
            computed.append(partial[t + 1])
        if t >= 3:
            product = down(t - 3)
            terms = product if terms is None else terms + product
            computed.append(terms)
        joined = list(lax.optimization_barrier(tuple(v for v in (faced, crossed, *computed) if v is not None)))
        faced = joined.pop(0)
        if crossed is not None:
            crossed = joined.pop(0)
        if t + 1 < count:
            partial[t + 1] = joined.pop(0)
        if joined:
            terms = joined.pop(0)
        if crossed is not None:
            own[t - 1] = activated(t - 1, sums[t - 1], crossed)
        sums[t] = (partial[t].astype(jnp.float32) + faced[:, : size[t]].astype(jnp.float32)).astype(jnp.bfloat16)
        if t >= 2:
            hidden[t - 2] = jnp.where(is_end, faced[:, : size[t - 2]], own[t - 2])
    faced = face(own[count - 2], facing)
    spans = (slice(half, None), slice(0, half))
    crossed = [cross(sums[count - 1][span]) for span in spans]
    stage(count, terms)
    terms = terms + down(count - 3)
    last = [activated(count - 1, sums[count - 1][spans[0]], crossed[0])]
    given = face(last[0], facing)
    crossed[1], _ = lax.optimization_barrier((crossed[1], last[0]))
    last.append(activated(count - 1, sums[count - 1][spans[1]], crossed[1]))
    kept = face(last[1], facing)
    hidden[count - 2] = jnp.where(is_end, faced, own[count - 2])
    terms = terms + down(count - 2)

    def finish(came, mine, before, weights):
        rows = jnp.where(is_end, came, mine)
        return before + jnp.dot(rows, weights, preferred_element_type=jnp.float32)

    given = finish(given, last[0], terms[half:], down_part[count - 1])
    return finish(kept, last[1], terms[:half], down_part[count]), given


def local(grid, inputs, ln_gain, ln_bias, w_up, up_bias, w_down, down_bias):
    width = inputs.shape[1] * grid.n_row
    early = []
    if grid.n_row == 4:
        row = lax.axis_index("row")
        is_end, w_first = lax.optimization_barrier((jnp.logical_or(row == 0, row == 3), w_up))
        edges = chunk_edges(w_up.shape[1])
        early.append(lax.optimization_barrier(lax.slice_in_dim(w_first, edges[0], edges[1], axis=1)))
    in_float = inputs.astype(jnp.float32)
    sums = jnp.stack([jnp.sum(in_float, axis=1), jnp.sum(in_float * in_float, axis=1)])
    total = row_sum(grid, sums)
    average = total[0] / width
    variance = total[1] / width - average * average
    normed = (in_float - average[:, None]) * lax.rsqrt(variance + 1e-05)[:, None]
    normed = (normed * ln_gain + ln_bias).astype(jnp.bfloat16)
    if grid.n_row == 4:
        early.append(cut(w_up, 1, edges[1], edges[2], normed))
    sooner, farthest = gather(grid, normed)
    if grid.n_row == 4:
        terms = four_rows(grid, is_end, early, sooner, farthest, w_up, up_bias, w_down)
    else:
        terms = chained_middle(grid, sooner, farthest, w_up, up_bias, w_down)
    down_sum = scatter_sum(grid, *terms)
    return (in_float + down_sum + down_bias).astype(jnp.bfloat16)


def solution(mesh):
    grid = Grid(mesh.shape["row"], mesh.shape["col"])
    placed = (
        P("col", "row"),
        P("row"),
        P("row"),
        P("row", "col"),
        P("col"),
        P("col", "row"),
        P("row"),
    )
    return jax.shard_map(
        functools.partial(local, grid), mesh=mesh, in_specs=placed, out_specs=P("col", "row"), check_vma=False
    )
```

```python
import functools
import math

import jax
import jax.numpy as jnp
from jax import lax
from jax.sharding import PartitionSpec as P


SHARES = (3, 3, 3, 3, 3, 3, 3, 3)
UP_AHEAD = 3
DOWN_AHEAD = 2


class Grid:
    def __init__(self, n_row, n_col):
        self.n_row, self.n_col = n_row, n_col
        self.cores = 2
        self.side = math.isqrt(n_col // self.cores)

    def shifted(self, index, dy, dx, dc):
        y, rest = divmod(index, self.side * self.cores)
        x, core = divmod(rest, self.cores)
        y, x = (y + dy) % self.side, (x + dx) % self.side
        core = (core + dc) % self.cores
        return (y * self.side + x) * self.cores + core

    def take(self, value, dy, dx, dc):
        pairs = [(self.shifted(i, dy, dx, dc), i) for i in range(self.n_col)]
        return lax.ppermute(value, "col", pairs)

    def give(self, value, dy, dx, dc):
        pairs = [(i, self.shifted(i, dy, dx, dc)) for i in range(self.n_col)]
        return lax.ppermute(value, "col", pairs)


def row_sum(grid, value):
    step = 1
    while step < grid.n_row:
        value = value + lax.ppermute(value, "row", [(i, i ^ step) for i in range(grid.n_row)])
        step *= 2
    return value


def gather(grid, own):
    held = [own]
    for k in range(1, grid.side * grid.side):
        held.append(grid.take(own, k // grid.side, k % grid.side, 0))
    return jnp.concatenate(held[:-1]), held[-1]


def scatter_sum(grid, kept, given):
    half = kept.shape[0]
    other = grid.give(given.astype(jnp.bfloat16), 0, 0, 1)
    pair = kept + other.astype(jnp.float32)
    rows = half // (grid.side * grid.side)
    total = pair[:rows]
    sent = pair.astype(jnp.bfloat16)
    for k in range(1, grid.side * grid.side):
        dy, dx = divmod(k, grid.side)
        total = total + grid.give(sent[k * rows : (k + 1) * rows], dy, dx, 0).astype(jnp.float32)
    return total


def chained_middle(grid, sooner, farthest, w_up, up_bias, w_down):
    n_row = grid.n_row
    held = jnp.concatenate([sooner, farthest])
    gathered = jnp.concatenate([held, grid.take(held, 0, 0, 1)])
    half = held.shape[0]
    row = lax.axis_index("row")
    middle = n_row // 2
    upper = row >= middle
    depth = jnp.where(upper, n_row - 1 - row, row)
    inward = [(i, i + 1) for i in range(middle - 1)] + [(i, i - 1) for i in range(middle + 1, n_row)]
    outward = [(j, i) for i, j in inward]
    across = [(middle - 1, middle), (middle, middle - 1)]
    acc = jnp.dot(gathered, w_up, preferred_element_type=jnp.float32).astype(jnp.bfloat16)
    partial = acc.astype(jnp.float32)
    for _ in range(middle - 1):
        acc = (partial + lax.ppermute(acc, "row", inward).astype(jnp.float32)).astype(jnp.bfloat16)
    crossed = lax.ppermute(jnp.where(upper, acc[:half], acc[half:]), "row", across)
    summed = jnp.where(upper, acc[half:], acc[:half]).astype(jnp.float32) + crossed.astype(jnp.float32)
    own = jax.nn.gelu(summed + up_bias, approximate=True).astype(jnp.bfloat16)
    other = lax.ppermute(own, "row", across)
    out = jnp.where(upper, jnp.concatenate([other, own]), jnp.concatenate([own, other]))
    for hop in range(middle - 1):
        got = lax.ppermute(out, "row", outward)
        out = jnp.where(depth == middle - 2 - hop, got, out)
    terms = jnp.dot(out, w_down, preferred_element_type=jnp.float32)
    return terms[:half], terms[half:]


def chunk_edges(units):
    pieces, edges = units // 128, [0]
    for share in SHARES:
        edges.append(edges[-1] + share)
    return [pieces * e // edges[-1] * 128 for e in edges]


def cut(weights, axis, low, high, after):
    weights, _ = lax.optimization_barrier((weights, after))
    return lax.optimization_barrier(lax.slice_in_dim(weights, low, high, axis=axis))


def four_rows(grid, is_end, early, sooner, farthest, w_up, up_bias, w_down):
    facing = [(0, 1), (1, 0), (2, 3), (3, 2)]
    across = []
    for i in range(grid.n_row * grid.n_col):
        own_row, own_col = divmod(i, grid.n_col)
        if own_row in (1, 2):
            across.append((i, (3 - own_row) * grid.n_col + own_col))
        else:
            across.append((i, own_row * grid.n_col + grid.shifted(own_col, 0, 0, 1)))
    edges = chunk_edges(w_up.shape[1])
    count = len(SHARES)
    size = [edges[k + 1] - edges[k] for k in range(count)]

    def face(sent, pairs):
        return lax.ppermute(sent, "row", pairs)

    def cross(sent):
        return lax.ppermute(sent, ("row", "col"), across)

    up_part, down_part = dict(enumerate(early)), {}

    def stage(t, after):
        k = t + UP_AHEAD
        if k < count and k not in up_part:
            up_part[k] = cut(w_up, 1, edges[k], edges[k + 1], after)
        k = t - 3 + DOWN_AHEAD
        if 0 <= k < count:
            down_part[k] = cut(w_down, 0, edges[k], edges[k + 1], after)
        if k == count - 1:
            down_part[count] = cut(w_down, 0, edges[k], edges[k + 1], down_part[k])

    def up(k):
        return jnp.dot(gathered, up_part[k], preferred_element_type=jnp.float32).astype(jnp.bfloat16)

    def down(k):
        return jnp.dot(hidden[k], down_part[k], preferred_element_type=jnp.float32)

    def activated(k, mine, came):
        summed = mine.astype(jnp.float32) + came.astype(jnp.float32) + up_bias[edges[k] : edges[k + 1]]
        return jax.nn.gelu(summed, approximate=True).astype(jnp.bfloat16)

    def widened(v, width):
        return v if v.shape[1] == width else jnp.pad(v, ((0, 0), (0, width - v.shape[1])))

    def up_first(v):
        return jnp.dot(v, up_part[0], preferred_element_type=jnp.float32).astype(jnp.bfloat16)

    first = [up_first(sooner)]
    farthest, first[0] = lax.optimization_barrier((farthest, first[0]))
    held = jnp.concatenate([sooner, farthest])
    half = held.shape[0]
    later = jnp.concatenate([farthest, grid.take(held, 0, 0, 1)])
    gathered = jnp.concatenate([sooner, later])
    first.append(up_first(later))
    for k in range(len(early), UP_AHEAD):
        up_part[k] = cut(w_up, 1, edges[k], edges[k + 1], gathered)
    partial, sums, own, hidden = {0: jnp.concatenate(first)}, {}, {}, {}
    terms = None

    faced = [face(v, facing) for v in first]
    stage(0, partial[0])
    partial[1] = up(1)
    ahead = face(partial[1], facing)
    faced, _ = lax.optimization_barrier((faced, partial[1]))
    parts = [(v.astype(jnp.float32) + came.astype(jnp.float32)).astype(jnp.bfloat16) for v, came in zip(first, faced)]
    crossed = [cross(v) for v in parts]
    stage(1, partial[1])
    partial[2] = up(2)
    ahead, crossed, partial[2] = lax.optimization_barrier((ahead, crossed, partial[2]))
    sums[0] = jnp.concatenate(parts)
    own[0] = activated(0, sums[0], jnp.concatenate(crossed))
    sums[1] = (partial[1].astype(jnp.float32) + ahead.astype(jnp.float32)).astype(jnp.bfloat16)
    for t in range(2, count):
        width = max(size[t], size[t - 2])
        faced = face(jnp.where(is_end, widened(partial[t], width), widened(own[t - 2], width)), facing)
        crossed = cross(sums[t - 1])
        stage(t, partial[t])
        computed = []
        if t + 1 < count:
            partial[t + 1] = up(t + 1)
            computed.append(partial[t + 1])
        if t >= 3:
            product = down(t - 3)
            terms = product if terms is None else terms + product
            computed.append(terms)
        joined = list(lax.optimization_barrier((faced, crossed, *computed)))
        faced, crossed = joined.pop(0), joined.pop(0)
        if t + 1 < count:
            partial[t + 1] = joined.pop(0)
        if joined:
            terms = joined.pop(0)
        own[t - 1] = activated(t - 1, sums[t - 1], crossed)
        sums[t] = (partial[t].astype(jnp.float32) + faced[:, : size[t]].astype(jnp.float32)).astype(jnp.bfloat16)
        hidden[t - 2] = jnp.where(is_end, faced[:, : size[t - 2]], own[t - 2])
    faced = face(own[count - 2], facing)
    spans = (slice(half, None), slice(0, half))
    crossed = [cross(sums[count - 1][span]) for span in spans]
    stage(count, terms)
    terms = terms + down(count - 3)
    last = [activated(count - 1, sums[count - 1][spans[0]], crossed[0])]
    given = face(last[0], facing)
    crossed[1], _ = lax.optimization_barrier((crossed[1], last[0]))
    last.append(activated(count - 1, sums[count - 1][spans[1]], crossed[1]))
    kept = face(last[1], facing)
    hidden[count - 2] = jnp.where(is_end, faced, own[count - 2])
    terms = terms + down(count - 2)

    def finish(came, mine, before, weights):
        rows = jnp.where(is_end, came, mine)
        return before + jnp.dot(rows, weights, preferred_element_type=jnp.float32)

    given = finish(given, last[0], terms[half:], down_part[count - 1])
    return finish(kept, last[1], terms[:half], down_part[count]), given


def local(grid, inputs, ln_gain, ln_bias, w_up, up_bias, w_down, down_bias):
    width = inputs.shape[1] * grid.n_row
    early = []
    if grid.n_row == 4:
        row = lax.axis_index("row")
        is_end, w_first = lax.optimization_barrier((jnp.logical_or(row == 0, row == 3), w_up))
        edges = chunk_edges(w_up.shape[1])
        early.append(lax.optimization_barrier(lax.slice_in_dim(w_first, edges[0], edges[1], axis=1)))
    in_float = inputs.astype(jnp.float32)
    sums = jnp.stack([jnp.sum(in_float, axis=1), jnp.sum(in_float * in_float, axis=1)])
    total = row_sum(grid, sums)
    average = total[0] / width
    variance = total[1] / width - average * average
    normed = (in_float - average[:, None]) * lax.rsqrt(variance + 1e-05)[:, None]
    normed = (normed * ln_gain + ln_bias).astype(jnp.bfloat16)
    if grid.n_row == 4:
        early.append(cut(w_up, 1, edges[1], edges[2], normed))
    sooner, farthest = gather(grid, normed)
    if grid.n_row == 4:
        terms = four_rows(grid, is_end, early, sooner, farthest, w_up, up_bias, w_down)
    else:
        terms = chained_middle(grid, sooner, farthest, w_up, up_bias, w_down)
    down_sum = scatter_sum(grid, *terms)
    return (in_float + down_sum + down_bias).astype(jnp.bfloat16)


def solution(mesh):
    grid = Grid(mesh.shape["row"], mesh.shape["col"])
    placed = (
        P("col", "row"),
        P("row"),
        P("row"),
        P("row", "col"),
        P("col"),
        P("col", "row"),
        P("row"),
    )
    return jax.shard_map(
        functools.partial(local, grid), mesh=mesh, in_specs=placed, out_specs=P("col", "row"), check_vma=False
    )
```
